256 devices in a mesh: tm: 128 (over y_lo, z, x, core), head: 2 (over y_hi).
Axes of the slice: x: 4, y: 4 (y_hi: 2, y_lo: 2; y = y_hi * 2 + y_lo), z: 8, core: 2. Of those that a mesh axis runs over, the one named last changes fastest.
Arguments:
- queries: bfloat16 [49152, 1536], P('tm', 'head'), may hold values from -160 to 160
- video_keys: bfloat16 [49152, 1536], P('tm', 'head'), may hold values from -6.5 to 6.5
- video_values: bfloat16 [49152, 1536], P('tm', 'head'), may hold values from -6 to 6
- prompt_keys: bfloat16 [256, 1536], P(None, 'head'), may hold values from -6 to 6
- prompt_values: bfloat16 [256, 1536], P(None, 'head'), may hold values from -6 to 6
- out_grad: bfloat16 [49152, 3072], P('tm', 'head'), may hold values from -6 to 6
- out_weight: bfloat16 [1536, 3072], P('head'), may hold values from -0.15625 to 0.15625
- windows: int32 [384, 2], replicated, may hold values from 0 to 3
- text_count: int32 [384], replicated, may hold values from 128 to 256
Outputs:
- query_grad: bfloat16 [49152, 1536], P('tm', 'head')
- key_grad: bfloat16 [49152, 1536], P('tm', 'head')
- value_grad: bfloat16 [49152, 1536], P('tm', 'head')
- prompt_key_grad: float32 [256, 1536], P(None, 'head')
- prompt_value_grad: float32 [256, 1536], P(None, 'head')
The draws below stay inside these ranges and needn't reach their ends.
All inputs are finite; a program needn't handle non-finite values.
Results may differ from the reference program's by a relative error of at most 0.0085.
Values may be sent and summed in bfloat16 or wider, within the bound.
A program may use at most 128 MiB of HBM per device.

```python
import jax
import jax.numpy as jnp
from jax import lax

D = 3072
HEADS = 12
HD = 128
TEXT = 256
TILE = 128
TOK_DEV = 384
VTOK = 49152
TILES = 384
N_TM = 128


def paired(key):
    base = jax.random.fold_in(key, 911)
    first, second = jax.random.split(base, 2)
    count = VTOK
    width = HEADS * HD
    keys = jnp.clip(jax.random.normal(first, (count, width), jnp.float32), -6.0, 6.0)
    query = jnp.clip(jax.random.normal(second, (count, width), jnp.float32), -6.0, 6.0)
    return (query, keys)


def draw_queries(key, part):
    return paired(key)[0].astype(jnp.bfloat16)


def draw_video_keys(key, part):
    return paired(key)[1].astype(jnp.bfloat16)


def touch_ends(values, own_key, least, high):
    index_at = [jax.random.randint(jax.random.fold_in(own_key, axis), (), 0, length) for axis, length in enumerate(values.shape)]
    main_axis = values.shape.index(max(values.shape))
    beside = index_at[:main_axis] + [(index_at[main_axis] + 1) % values.shape[main_axis]] + index_at[main_axis + 1:]
    return values.at[tuple(index_at)].set(least).at[tuple(beside)].set(high)


def level_of(rng, shape, cuts, smallest, largest):
    def one(dim, shards_of):
        draws = jax.random.uniform(jax.random.fold_in(jax.random.fold_in(rng, 6), dim), (shards_of,), jnp.float32, smallest / len(cuts), largest / len(cuts))
        return jnp.repeat(jnp.exp(draws), shape[dim] // shards_of).reshape((-1,) + (1,) * (len(shape) - dim - 1))

    level = one(*cuts[0])
    for cut in cuts[1:]:
        level = level * one(*cut)
    return level


def bell_draw(key, dims, deviation, most, cuts=(), kind=jnp.bfloat16):
    values = jax.random.normal(key, dims, jnp.float32) * deviation
    if len(cuts) > 0:
        values = level_of(key, dims, cuts, -0.22, 0.18) * values
    return jnp.clip(values, min=-most, max=most).astype(kind)


def setup_inputs(seed: int = 0) -> dict:
    seeds = jax.random.split(jax.random.key(seed), 10)
    return {
        "queries": draw_queries(jax.random.fold_in(seeds[9], 71), 0),
        "video_keys": draw_video_keys(jax.random.fold_in(seeds[9], 71), 0),
        "video_values": bell_draw(seeds[2], (VTOK, HEADS * HD), 1.0, 6.0, ((0, 128), (1, 2))),
        "prompt_keys": bell_draw(seeds[3], (TEXT, HEADS * HD), 1.0, 6.0, ((1, 2),)),
        "prompt_values": bell_draw(seeds[4], (TEXT, HEADS * HD), 1.0, 6.0, ((1, 2),)),
        "out_grad": bell_draw(seeds[5], (VTOK, D), 1.0, 6.0, ((0, 128), (1, 2))),
        "out_weight": bell_draw(seeds[6], (HEADS * HD, D), (HEADS * HD) ** -0.5, 0.15625, ((0, 2),)),
        "windows": touch_ends(jax.random.randint(seeds[7], (TILES, 2), 0, TOK_DEV // TILE + 1), jax.random.fold_in(seeds[7], 1), 0, (TOK_DEV // TILE + 1) - 1).astype(jnp.int32),
        "text_count": touch_ends(jax.random.randint(seeds[8], (TILES,), TEXT // 2, TEXT + 1), jax.random.fold_in(seeds[8], 1), TEXT // 2, TEXT).astype(jnp.int32),
    }


def reference(queries, video_keys, video_values, prompt_keys, prompt_values, out_grad, out_weight, windows, text_count):
    scale = HD ** -0.5
    slabs = N_TM
    rows = TOK_DEV
    tiles = TOK_DEV // TILE
    width = HEADS * HD
    attn_grad = jnp.dot(out_grad, out_weight.T, preferred_element_type=jnp.float32).astype(jnp.bfloat16)
    local_tile = jnp.arange(rows, dtype=jnp.int32) // TILE
    video_tile = jnp.arange(3 * rows, dtype=jnp.int32) // TILE - tiles
    text_index = jnp.arange(TEXT, dtype=jnp.int32)

    def rows_of(array, index):
        return lax.dynamic_slice_in_dim(array, (index * rows).astype(jnp.int32), rows, 0)

    def step(carry, slab):
        key_acc, value_acc, text_key, text_value = carry
        before = (slab + slabs - 1) % slabs
        after = (slab + 1) % slabs
        query = rows_of(queries, slab).astype(jnp.float32).reshape(rows, HEADS, HD)
        keys = jnp.concatenate([rows_of(video_keys, before), rows_of(video_keys, slab), rows_of(video_keys, after), prompt_keys], 0)
        values = jnp.concatenate([rows_of(video_values, before), rows_of(video_values, slab), rows_of(video_values, after), prompt_values], 0)
        keys = keys.astype(jnp.float32).reshape(-1, HEADS, HD)
        values = values.astype(jnp.float32).reshape(-1, HEADS, HD)
        grad = rows_of(attn_grad, slab).astype(jnp.float32).reshape(rows, HEADS, HD)
        part = lax.dynamic_slice_in_dim(windows, (slab * tiles).astype(jnp.int32), tiles, 0)
        limit = jnp.repeat(lax.dynamic_slice_in_dim(text_count, (slab * tiles).astype(jnp.int32), tiles, 0), TILE)
        back = jnp.repeat(part[:, 0], TILE)
        ahead = jnp.repeat(part[:, 1], TILE)
        offset = video_tile[None, :] - local_tile[:, None]
        video_mask = (offset >= -back[:, None]) & (offset <= ahead[:, None])
        text_mask = text_index[None, :] < limit[:, None]
        mask = jnp.concatenate([video_mask, text_mask], 1)
        scores = jnp.einsum("qhd,khd->hqk", query, keys, precision=lax.Precision.HIGHEST) * scale
        scores = jnp.where(mask[None], scores, -jnp.inf)
        top = jnp.max(scores, -1, keepdims=True)
        weight = jnp.exp(scores - top)
        total = jnp.sum(weight, -1, keepdims=True)
        prob = weight / total
        prob_half = lax.optimization_barrier(prob.astype(jnp.bfloat16)).astype(jnp.float32)
        attended = jnp.einsum("hqk,khd->qhd", prob_half, values, precision=lax.Precision.HIGHEST)
        delta = jnp.sum(grad * attended, -1)
        dprob = jnp.einsum("qhd,khd->hqk", grad, values, precision=lax.Precision.HIGHEST)
        dscore = prob * (dprob - delta.T[:, :, None])
        dscore = lax.optimization_barrier(dscore.astype(jnp.bfloat16)).astype(jnp.float32)
        query_grad = (jnp.einsum("hqk,khd->qhd", dscore, keys, precision=lax.Precision.HIGHEST) * scale).reshape(rows, width)
        key_term = (jnp.einsum("hqk,qhd->khd", dscore, query, precision=lax.Precision.HIGHEST) * scale).reshape(-1, width)
        value_term = jnp.einsum("hqk,qhd->khd", prob_half, grad, precision=lax.Precision.HIGHEST).reshape(-1, width)
        for number, index in enumerate([before, slab, after]):
            start = (index * rows).astype(jnp.int32)
            key_acc = lax.dynamic_update_slice_in_dim(key_acc, rows_of(key_acc, index) + key_term[number * rows:(number + 1) * rows], start, 0)
            value_acc = lax.dynamic_update_slice_in_dim(value_acc, rows_of(value_acc, index) + value_term[number * rows:(number + 1) * rows], start, 0)
        text_key = text_key + key_term[3 * rows:]
        text_value = text_value + value_term[3 * rows:]
        return (key_acc, value_acc, text_key, text_value), query_grad.astype(jnp.bfloat16)

    start_state = (jnp.zeros((VTOK, width), jnp.float32), jnp.zeros((VTOK, width), jnp.float32),
                   jnp.zeros((TEXT, width), jnp.float32), jnp.zeros((TEXT, width), jnp.float32))
    final, query_blocks = lax.scan(step, start_state, jnp.arange(slabs, dtype=jnp.int32))
    key_acc, value_acc, text_key, text_value = final
    return (query_blocks.reshape(VTOK, width), key_acc.astype(jnp.bfloat16), value_acc.astype(jnp.bfloat16), text_key, text_value)
```

```python
import jax
import jax.numpy as jnp
from jax import lax
from jax.experimental import pallas as pl
from jax.experimental.pallas import tpu as pltpu
from jax.sharding import PartitionSpec as P

HD = 128
TILE = 128
HEADS = 6
ROWS = 384
WIDTH = HEADS * HD
TEXT = 256
HALF = 1536
SEEN = 7 * TILE
KEYS = 9 * TILE
NEG = -1e30
SCALE = HD**-0.5
MESH = pl.DeviceIdType.MESH

OG, KV, CC, XX, ZZ, YY, ZG, XG, CG, PP, SLOTS = 0, 3, 7, 8, 11, 18, 19, 26, 29, 33, 35


def nt(a, b):
    return lax.dot_general(a, b, (((1,), (1,)), ((), ())), preferred_element_type=jnp.float32)


def tn(a, b):
    return lax.dot_general(a, b, (((0,), (0,)), ((), ())), preferred_element_type=jnp.float32)


def nn(a, b):
    return jnp.dot(a, b, preferred_element_type=jnp.float32)


def folded(x, op):
    return op(x.reshape(TILE // 8, 8, HD), axis=0)


def kernel(
    windows, counts, q_in, k_in, v_in, pk_in, pv_in, og_in, w_in,
    dq_out, dk_out, dv_out, tk_out, tv_out,
    qbuf, kbuf, vbuf, ogown, ogoth, wown, woth, gpart, gbuf, prob, inv, dp, half, dsc, kacc, vacc, tacc,
    csend, crecv, tsum, xsend, xrecv, zsum, zsend, zrecv, ysend, yrecv, allg, psend, precv,
    loc, ssem, rsem,
):
    tm, head = lax.axis_index("tm"), lax.axis_index("head")
    core, x, z, y = tm % 2, (tm // 2) % 4, (tm // 8) % 8, tm // 64

    def at(y_, z_, x_):
        return (((y_ * 8 + z_) * 4 + x_) * 2 + core, head)

    partner = (tm, 1 - head)
    before, after = ((tm + 127) % 128, head), ((tm + 1) % 128, head)
    twin = (tm + 1 - 2 * core, head)
    xs = [at(y, z, (x + k) % 4) for k in range(1, 4)]
    zs = [at(y, (z + k) % 8, x) for k in range(1, 8)]
    other_y = at(1 - y, z, x)

    def local(n, src, dst):
        copy = pltpu.make_async_copy(src, dst, loc.at[n])
        copy.start()
        return copy

    def send(n, src, dst, device):
        copy = pltpu.make_async_remote_copy(
            src_ref=src, dst_ref=dst, send_sem=ssem.at[n], recv_sem=rsem.at[n],
            device_id=device, device_id_type=MESH,
        )
        copy.start()
        return copy

    mine = pl.ds(pl.multiple_of(head * HALF, HALF), HALF)
    theirs = pl.ds(pl.multiple_of((1 - head) * HALF, HALF), HALF)
    l_og = local(0, og_in, ogown)
    l_w = local(1, w_in.at[:, mine], wown)
    l_q = local(2, q_in, qbuf)
    l_k = local(3, k_in, kbuf.at[pl.ds(ROWS, ROWS)])
    l_pk = local(4, pk_in, kbuf.at[pl.ds(3 * ROWS, TEXT)])
    l_v = local(5, v_in, vbuf.at[pl.ds(ROWS, ROWS)])
    l_pv = local(6, pv_in, vbuf.at[pl.ds(3 * ROWS, TEXT)])
    l_w2 = local(7, w_in.at[:, theirs], woth)

    barrier = pltpu.get_barrier_semaphore()
    peers = [partner, before, after, *xs, *zs, other_y]
    for peer in peers:
        pl.semaphore_signal(barrier, inc=1, device_id=peer, device_id_type=MESH)
    pl.semaphore_wait(barrier, len(peers))

    ogs = [
        send(OG + i, og_in.at[pl.ds(i * TILE, TILE)], ogoth.at[pl.ds(i * TILE, TILE)], partner)
        for i in range(3)
    ]
    kvs = [
        send(KV + 0, k_in, kbuf.at[pl.ds(0, ROWS)], after),
        send(KV + 1, k_in, kbuf.at[pl.ds(2 * ROWS, ROWS)], before),
        send(KV + 2, v_in, vbuf.at[pl.ds(0, ROWS)], after),
        send(KV + 3, v_in, vbuf.at[pl.ds(2 * ROWS, ROWS)], before),
    ]

    kacc[...] = jnp.zeros_like(kacc)
    vacc[...] = jnp.zeros_like(vacc)
    tacc[...] = jnp.zeros_like(tacc)

    l_og.wait()
    l_w.wait()

    def project_own(h, carry):
        cols = pl.ds(pl.multiple_of(h * HD, HD), HD)
        gpart[:, cols] = nt(ogown[...], wown[cols, :])
        return carry

    lax.fori_loop(0, HEADS, project_own, 0)

    for copy in (l_q, l_k, l_pk):
        copy.wait()
    kvs[0].wait()
    kvs[1].wait()

    def weights(n, carry):
        i, h = n // HEADS, n % HEADS
        cols = pl.ds(pl.multiple_of(h * HD, HD), HD)
        q = qbuf[pl.ds(pl.multiple_of(i * TILE, TILE), TILE), cols]
        back, ahead, count = windows[tm * 3 + i, 0], windows[tm * 3 + i, 1], counts[tm * 3 + i]
        prob[n, pl.ds(0, SEEN), :] = nt(kbuf[pl.ds(pl.multiple_of(i * TILE, TILE), SEEN), cols], q)
        prob[n, pl.ds(SEEN, TEXT), :] = nt(kbuf[pl.ds(3 * ROWS, TEXT), cols], q)
        row = lax.broadcasted_iota(jnp.int32, (TILE, HD), 0)
        biases = []
        top = jnp.full((8, HD), NEG, jnp.float32)
        for j in range(9):
            block = prob[n, pl.ds(j * TILE, TILE), :]
            if j < 7:
                bias = jnp.where((j - 3 >= -back) & (j - 3 <= ahead), 0.0, NEG).astype(jnp.float32)
                biases.append(bias)
                top = jnp.maximum(top, folded(block, jnp.max) + bias)
            else:
                block = jnp.where(row + (j - 7) * TILE < count, block, NEG)
                prob[n, pl.ds(j * TILE, TILE), :] = block
                top = jnp.maximum(top, folded(block, jnp.max))
        top = jnp.max(top, axis=0, keepdims=True)
        total = jnp.zeros((8, HD), jnp.float32)
        for j in range(9):
            shift = top - biases[j] if j < 7 else top
            weight = jnp.exp((prob[n, pl.ds(j * TILE, TILE), :] - shift) * SCALE)
            prob[n, pl.ds(j * TILE, TILE), :] = weight
            total += folded(weight, jnp.sum)
        inv[n] = jnp.broadcast_to(1.0 / jnp.sum(total, axis=0, keepdims=True), (8, HD))
        return carry

    lax.fori_loop(0, 3 * HEADS, weights, 0)

    for copy in (l_v, l_pv, l_w2):
        copy.wait()
    kvs[2].wait()
    kvs[3].wait()

    def project_rest(i, h):
        rows = pl.ds(i * TILE, TILE)
        cols = pl.ds(pl.multiple_of(h * HD, HD), HD)
        g = gpart[rows, cols] + nt(ogoth[rows, :], woth[cols, :])
        gbuf[rows, cols] = g.astype(jnp.bfloat16)

    def scores_back(i, h):
        n = i * HEADS + h
        rows = pl.ds(i * TILE, TILE)
        cols = pl.ds(pl.multiple_of(h * HD, HD), HD)
        g = gbuf[rows, cols]
        dp[pl.ds(0, SEEN), :] = nt(vbuf[pl.ds(i * TILE, SEEN), cols], g)
        dp[pl.ds(SEEN, TEXT), :] = nt(vbuf[pl.ds(3 * ROWS, TEXT), cols], g)
        scale = inv[n][0:1]
        delta = jnp.zeros((8, HD), jnp.float32)
        for j in range(9):
            part = pl.ds(j * TILE, TILE)
            p = prob[n, part, :] * scale
            prob[n, part, :] = p
            p16 = p.astype(jnp.bfloat16)
            half[h, part, :] = p16
            delta += folded(p16.astype(jnp.float32) * dp[part, :], jnp.sum)
        delta = jnp.sum(delta, axis=0, keepdims=True)
        for j in range(9):
            part = pl.ds(j * TILE, TILE)
            dsc[h, part, :] = (prob[n, part, :] * (dp[part, :] - delta)).astype(jnp.bfloat16)
        tacc[0, :, cols] += nn(dsc[h, pl.ds(SEEN, TEXT), :], qbuf[rows, cols])
        tacc[1, :, cols] += nn(half[h, pl.ds(SEEN, TEXT), :], g)

    def grads_back(i, h):
        rows = pl.ds(i * TILE, TILE)
        cols = pl.ds(pl.multiple_of(h * HD, HD), HD)
        seen = pl.ds(i * TILE, SEEN)
        vacc[seen, cols] += nn(half[h, pl.ds(0, SEEN), :], gbuf[rows, cols])
        kacc[seen, cols] += nn(dsc[h, pl.ds(0, SEEN), :], qbuf[rows, cols])
        grad = tn(dsc[h, pl.ds(0, SEEN), :], kbuf[seen, cols])
        grad += tn(dsc[h, pl.ds(SEEN, TEXT), :], kbuf[pl.ds(3 * ROWS, TEXT), cols])
        dq_out[rows, cols] = (grad * SCALE).astype(jnp.bfloat16)

    def each_head(step, i, first=0, last=HEADS):
        def body(h, carry):
            step(i, h)
            return carry

        lax.fori_loop(first, last, body, 0)

    for i in range(3):
        ogs[i].wait()
        each_head(project_rest, i)
        each_head(scores_back, i)
        if i < 2:
            each_head(grads_back, i)

    csend[...] = tacc[1 - core].astype(jnp.bfloat16)
    c_copy = send(CC, csend, crecv, twin)
    each_head(grads_back, 2, 0, 3)
    c_copy.wait()
    total = tacc[core] + crecv[...].astype(jnp.float32)
    tsum[...] = total
    xsend[...] = total.astype(jnp.bfloat16)
    x_copies = [
        send(
            XX + k - 1,
            xsend.at[pl.ds(pl.multiple_of((x + k) % 4 * 64, 64), 64)],
            xrecv.at[k - 1],
            xs[k - 1],
        )
        for k in range(1, 4)
    ]
    each_head(grads_back, 2, 3, HEADS)
    for kind, acc in ((0, kacc), (1, vacc)):
        psend[0, kind] = acc[pl.ds(0, ROWS), :].astype(jnp.bfloat16)
        psend[1, kind] = acc[pl.ds(2 * ROWS, ROWS), :].astype(jnp.bfloat16)
    for copy in x_copies:
        copy.wait()
    total = tsum[pl.ds(pl.multiple_of(x * 64, 64), 64), :]
    for k in range(3):
        total += xrecv[k].astype(jnp.float32)
    for n in range(8):
        piece = total[n // 2 * 16 : n // 2 * 16 + 16, n % 2 * 384 : n % 2 * 384 + 384]
        zsum[n] = piece
        zsend[n] = piece.astype(jnp.bfloat16)
    z_copies = [
        send(ZZ + k - 1, zsend.at[(z + k) % 8], zrecv.at[k - 1], zs[k - 1]) for k in range(1, 8)
    ]
    p_copies = [
        send(PP + 0, psend.at[0], precv.at[0], before),
        send(PP + 1, psend.at[1], precv.at[1], after),
    ]
    for copy in z_copies:
        copy.wait()
    total = zsum[z]
    for k in range(7):
        total += zrecv[k].astype(jnp.float32)
    ysend[...] = total
    y_copy = send(YY, ysend, yrecv, other_y)
    y_copy.wait()
    allg[core, x, z] = (ysend[...] + yrecv[...]).astype(jnp.bfloat16)
    zg = [
        send(ZG + k - 1, allg.at[core, x, z], allg.at[core, x, z], zs[k - 1]) for k in range(1, 8)
    ]
    for copy in zg:
        copy.wait()
    xg = [send(XG + k - 1, allg.at[core, x], allg.at[core, x], xs[k - 1]) for k in range(1, 4)]
    cg = [send(CG, allg.at[core, x], allg.at[core, x], twin)]
    for k in range(1, 4):
        xg[k - 1].wait()
        there = (x + 4 - k) % 4
        cg.append(send(CG + k, allg.at[core, there], allg.at[core, there], twin))
    for copy in p_copies:
        copy.wait()
    for kind, acc, out, factor in ((0, kacc, dk_out, SCALE), (1, vacc, dv_out, 1.0)):
        grad = acc[pl.ds(ROWS, ROWS), :] + precv[0, kind].astype(jnp.float32)
        grad += precv[1, kind].astype(jnp.float32)
        out[...] = (grad * factor).astype(jnp.bfloat16)
    for copy in cg:
        copy.wait()
    for kind, out, factor in ((0, tk_out, SCALE), (1, tv_out, 1.0)):
        for xi in range(4):
            for n in range(8):
                piece = allg[kind, xi, n].astype(jnp.float32) * factor
                out[pl.ds(xi * 64 + n // 2 * 16, 16), pl.ds(n % 2 * 384, 384)] = piece


def per_device(queries, video_keys, video_values, prompt_keys, prompt_values, out_grad, out_weight, windows, counts):
    f32, bf16 = jnp.float32, jnp.bfloat16
    hbm = pl.BlockSpec(memory_space=pl.ANY)
    smem = pl.BlockSpec(memory_space=pltpu.SMEM)
    vmem = pl.BlockSpec(memory_space=pltpu.VMEM)
    V = pltpu.VMEM
    return pl.pallas_call(
        kernel,
        out_shape=[jax.ShapeDtypeStruct((ROWS, WIDTH), bf16)] * 3 + [jax.ShapeDtypeStruct((TEXT, WIDTH), f32)] * 2,
        in_specs=[smem, smem] + [hbm] * 7,
        out_specs=[vmem] * 5,
        scratch_shapes=[
            V((ROWS, WIDTH), bf16),
            V((3 * ROWS + TEXT, WIDTH), bf16),
            V((3 * ROWS + TEXT, WIDTH), bf16),
            V((ROWS, HALF), bf16),
            V((ROWS, HALF), bf16),
            V((WIDTH, HALF), bf16),
            V((WIDTH, HALF), bf16),
            V((ROWS, WIDTH), f32),
            V((ROWS, WIDTH), bf16),
            V((3 * HEADS, KEYS, HD), f32),
            V((3 * HEADS, 8, HD), f32),
            V((KEYS, HD), f32),
            V((HEADS, KEYS, HD), bf16),
            V((HEADS, KEYS, HD), bf16),
            V((3 * ROWS, WIDTH), f32),
            V((3 * ROWS, WIDTH), f32),
            V((2, TEXT, WIDTH), f32),
            V((TEXT, WIDTH), bf16),
            V((TEXT, WIDTH), bf16),
            V((TEXT, WIDTH), f32),
            V((TEXT, WIDTH), bf16),
            V((3, 64, WIDTH), bf16),
            V((8, 16, 384), f32),
            V((8, 16, 384), bf16),
            V((7, 16, 384), bf16),
            V((16, 384), f32),
            V((16, 384), f32),
            V((2, 4, 8, 16, 384), bf16),
            V((2, 2, ROWS, WIDTH), bf16),
            V((2, 2, ROWS, WIDTH), bf16),
            pltpu.SemaphoreType.DMA((8,)),
            pltpu.SemaphoreType.DMA((SLOTS,)),
            pltpu.SemaphoreType.DMA((SLOTS,)),
        ],
        compiler_params=pltpu.CompilerParams(
            collective_id=0, has_side_effects=True, vmem_limit_bytes=63 << 20
        ),
        name="step",
    )(windows, counts, queries, video_keys, video_values, prompt_keys, prompt_values, out_grad, out_weight)


def solution(mesh):
    both = P("tm", "head")
    text = P(None, "head")
    return jax.shard_map(
        per_device,
        mesh=mesh,
        in_specs=(both, both, both, text, text, both, P("head", None), P(None, None), P(None)),
        out_specs=(both, both, both, text, text),
        check_vma=False,
    )
```

```python
import jax
import jax.numpy as jnp
from jax import lax
from jax.experimental import pallas as pl
from jax.experimental.pallas import tpu as pltpu
from jax.sharding import PartitionSpec as P

HD = 128
PAIR = 2 * HD
TILE = 128
HEADS = 6
ROWS = 384
WIDTH = HEADS * HD
TEXT = 256
HALF = 1536
SEEN = 7 * TILE
KEYS = 9 * TILE
NEG = -1e30
SCALE = HD**-0.5
MESH = pl.DeviceIdType.MESH

OG, KV, CC, XX, ZZ, YY, ZG, XG, CG, PP, SLOTS = 0, 3, 7, 8, 11, 18, 19, 26, 29, 33, 43


def nt(a, b):
    return lax.dot_general(a, b, (((1,), (1,)), ((), ())), preferred_element_type=jnp.float32)


def tn(a, b):
    return lax.dot_general(a, b, (((0,), (0,)), ((), ())), preferred_element_type=jnp.float32)


def nn(a, b):
    return jnp.dot(a, b, preferred_element_type=jnp.float32)


def folded(x, op):
    return op(x.reshape(TILE // 8, 8, HD), axis=0)


def kernel(
    windows, counts, q_in, k_in, v_in, pk_in, pv_in, og_in, w_in,
    dq_out, dk_out, dv_out, tk_out, tv_out,
    qbuf, kbuf, vbuf, ogown, ogoth, wown, woth, gpart, gbuf, prob, inv, dp, half, dsc, kacc, vacc, tacc,
    csend, crecv, tsum, xsend, xrecv, zsum, zsend, zrecv, ysend, yrecv, allg, psend, precv,
    loc, ssem, rsem,
):
    tm, head = lax.axis_index("tm"), lax.axis_index("head")
    core, x, z, y = tm % 2, (tm // 2) % 4, (tm // 8) % 8, tm // 64

    def at(y_, z_, x_):
        return (((y_ * 8 + z_) * 4 + x_) * 2 + core, head)

    partner = (tm, 1 - head)
    before, after = ((tm + 127) % 128, head), ((tm + 1) % 128, head)
    twin = (tm + 1 - 2 * core, head)
    xs = [at(y, z, (x + k) % 4) for k in range(1, 4)]
    zs = [at(y, (z + k) % 8, x) for k in range(1, 8)]
    other_y = at(1 - y, z, x)

    def local(n, src, dst):
        copy = pltpu.make_async_copy(src, dst, loc.at[n])
        copy.start()
        return copy

    def send(n, src, dst, device):
        copy = pltpu.make_async_remote_copy(
            src_ref=src, dst_ref=dst, send_sem=ssem.at[n], recv_sem=rsem.at[n],
            device_id=device, device_id_type=MESH,
        )
        copy.start()
        return copy

    mine = pl.ds(pl.multiple_of(head * HALF, HALF), HALF)
    theirs = pl.ds(pl.multiple_of((1 - head) * HALF, HALF), HALF)
    l_og = local(0, og_in, ogown)
    l_w = local(1, w_in.at[:, mine], wown)
    l_q = local(2, q_in, qbuf)
    l_k = local(3, k_in, kbuf.at[pl.ds(ROWS, ROWS)])
    l_pk = local(4, pk_in, kbuf.at[pl.ds(3 * ROWS, TEXT)])
    l_v = local(5, v_in, vbuf.at[pl.ds(ROWS, ROWS)])
    l_pv = local(6, pv_in, vbuf.at[pl.ds(3 * ROWS, TEXT)])
    l_w2 = local(7, w_in.at[:, theirs], woth)

    barrier = pltpu.get_barrier_semaphore()
    peers = [partner, before, after, *xs, *zs, other_y]
    for peer in peers:
        pl.semaphore_signal(barrier, inc=1, device_id=peer, device_id_type=MESH)
    pl.semaphore_wait(barrier, len(peers))

    ogs = [
        send(OG + i, og_in.at[pl.ds(i * TILE, TILE)], ogoth.at[pl.ds(i * TILE, TILE)], partner)
        for i in range(3)
    ]
    kvs = [
        send(KV + 0, k_in, kbuf.at[pl.ds(0, ROWS)], after),
        send(KV + 1, k_in, kbuf.at[pl.ds(2 * ROWS, ROWS)], before),
        send(KV + 2, v_in, vbuf.at[pl.ds(0, ROWS)], after),
        send(KV + 3, v_in, vbuf.at[pl.ds(2 * ROWS, ROWS)], before),
    ]

    kacc[...] = jnp.zeros_like(kacc)
    vacc[...] = jnp.zeros_like(vacc)
    tacc[...] = jnp.zeros_like(tacc)

    l_og.wait()
    l_w.wait()

    def project_own(h, carry):
        cols = pl.ds(pl.multiple_of(h * PAIR, PAIR), PAIR)
        gpart[:, cols] = nt(ogown[...], wown[cols, :])
        return carry

    lax.fori_loop(0, HEADS // 2, project_own, 0)

    for copy in (l_q, l_k, l_pk):
        copy.wait()
    kvs[0].wait()
    kvs[1].wait()

    def weights(n, carry):
        i, h = n // HEADS, n % HEADS
        cols = pl.ds(pl.multiple_of(h * HD, HD), HD)
        q = qbuf[pl.ds(pl.multiple_of(i * TILE, TILE), TILE), cols]
        back, ahead, count = windows[0, tm * 3 + i], windows[1, tm * 3 + i], counts[tm * 3 + i]
        prob[n, pl.ds(0, SEEN), :] = nt(kbuf[pl.ds(pl.multiple_of(i * TILE, TILE), SEEN), cols], q)
        prob[n, pl.ds(SEEN, TEXT), :] = nt(kbuf[pl.ds(3 * ROWS, TEXT), cols], q)
        row = lax.broadcasted_iota(jnp.int32, (TILE, HD), 0)
        biases = []
        top = jnp.full((8, HD), NEG, jnp.float32)
        for j in range(9):
            block = prob[n, pl.ds(j * TILE, TILE), :]
            if j < 7:
                bias = jnp.where((j - 3 >= -back) & (j - 3 <= ahead), 0.0, NEG).astype(jnp.float32)
                biases.append(bias)
                top = jnp.maximum(top, folded(block, jnp.max) + bias)
            else:
                block = jnp.where(row + (j - 7) * TILE < count, block, NEG)
                prob[n, pl.ds(j * TILE, TILE), :] = block
                top = jnp.maximum(top, folded(block, jnp.max))
        top = jnp.max(top, axis=0, keepdims=True)
        total = jnp.zeros((8, HD), jnp.float32)
        for j in range(9):
            shift = top - biases[j] if j < 7 else top
            weight = jnp.exp((prob[n, pl.ds(j * TILE, TILE), :] - shift) * SCALE)
            prob[n, pl.ds(j * TILE, TILE), :] = weight
            total += folded(weight, jnp.sum)
        inv[n] = jnp.broadcast_to(1.0 / jnp.sum(total, axis=0, keepdims=True), (8, HD))
        return carry

    lax.fori_loop(0, 3 * HEADS, weights, 0)

    for copy in (l_v, l_pv, l_w2):
        copy.wait()
    kvs[2].wait()
    kvs[3].wait()

    def project_rest(i, h):
        rows = pl.ds(i * TILE, TILE)
        cols = pl.ds(pl.multiple_of(h * PAIR, PAIR), PAIR)
        g = gpart[rows, cols] + nt(ogoth[rows, :], woth[cols, :])
        gbuf[rows, cols] = g.astype(jnp.bfloat16)

    def scores_back(i, h):
        n = i * HEADS + h
        rows = pl.ds(i * TILE, TILE)
        cols = pl.ds(pl.multiple_of(h * HD, HD), HD)
        g = gbuf[rows, cols]
        dp[pl.ds(0, SEEN), :] = nt(vbuf[pl.ds(i * TILE, SEEN), cols], g)
        dp[pl.ds(SEEN, TEXT), :] = nt(vbuf[pl.ds(3 * ROWS, TEXT), cols], g)
        scale = inv[n][0:1]
        delta = jnp.zeros((8, HD), jnp.float32)
        for j in range(9):
            part = pl.ds(j * TILE, TILE)
            p = prob[n, part, :] * scale
            prob[n, part, :] = p
            p16 = p.astype(jnp.bfloat16)
            half[h, part, :] = p16
            delta += folded(p16.astype(jnp.float32) * dp[part, :], jnp.sum)
        delta = jnp.sum(delta, axis=0, keepdims=True)
        for j in range(9):
            part = pl.ds(j * TILE, TILE)
            dsc[h, part, :] = (prob[n, part, :] * (dp[part, :] - delta)).astype(jnp.bfloat16)
        tacc[0, :, cols] += nn(dsc[h, pl.ds(SEEN, TEXT), :], qbuf[rows, cols])
        tacc[1, :, cols] += nn(half[h, pl.ds(SEEN, TEXT), :], g)

    def grads_back(i, h):
        rows = pl.ds(i * TILE, TILE)
        cols = pl.ds(pl.multiple_of(h * HD, HD), HD)
        seen = pl.ds(i * TILE, SEEN)
        vacc[seen, cols] += nn(half[h, pl.ds(0, SEEN), :], gbuf[rows, cols])
        kacc[seen, cols] += nn(dsc[h, pl.ds(0, SEEN), :], qbuf[rows, cols])
        grad = tn(dsc[h, pl.ds(0, SEEN), :], kbuf[seen, cols])
        grad += tn(dsc[h, pl.ds(SEEN, TEXT), :], kbuf[pl.ds(3 * ROWS, TEXT), cols])
        dq_out[rows, cols] = (grad * SCALE).astype(jnp.bfloat16)

    def each_head(step, i, first=0, last=HEADS):
        def body(h, carry):
            step(i, h)
            return carry

        lax.fori_loop(first, last, body, 0)

    p_copies = []

    def pack(side, source, start, count):
        for kind, acc in ((0, kacc), (1, vacc)):
            psend[side, kind, pl.ds(start, count), :] = acc[pl.ds(source, count), :].astype(jnp.bfloat16)

    def send_part(side, start, count):
        part = pl.ds(start, count)
        return send(
            PP + len(p_copies), psend.at[side, :, part], precv.at[side, :, part], after if side else before
        )

    for i in range(3):
        ogs[i].wait()
        each_head(project_rest, i, 0, HEADS // 2)
        each_head(scores_back, i)
        if i < 2:
            each_head(grads_back, i)
            pack(0, i * TILE, i * TILE, TILE)
            p_copies.append(send_part(0, i * TILE, TILE))

    csend[...] = tacc[1 - core].astype(jnp.bfloat16)
    c_copy = send(CC, csend, crecv, twin)
    each_head(grads_back, 2, 0, 3)
    c_copy.wait()
    total = tacc[core] + crecv[...].astype(jnp.float32)
    tsum[...] = total
    xsend[...] = total.astype(jnp.bfloat16)
    x_copies = [
        send(
            XX + k - 1,
            xsend.at[pl.ds(pl.multiple_of((x + k) % 4 * 64, 64), 64)],
            xrecv.at[k - 1],
            xs[k - 1],
        )
        for k in range(1, 4)
    ]
    each_head(grads_back, 2, 3, HEADS)
    pack(0, 2 * TILE, 2 * TILE, TILE)
    pack(1, 2 * ROWS, 0, ROWS)
    for copy in x_copies:
        copy.wait()
    total = tsum[pl.ds(pl.multiple_of(x * 64, 64), 64), :]
    for k in range(3):
        total += xrecv[k].astype(jnp.float32)
    for n in range(8):
        piece = total[n // 2 * 16 : n // 2 * 16 + 16, n % 2 * 384 : n % 2 * 384 + 384]
        zsum[n] = piece
        zsend[n] = piece.astype(jnp.bfloat16)
    z_copies = [
        send(ZZ + k - 1, zsend.at[(z + k) % 8], zrecv.at[k - 1], zs[k - 1]) for k in range(1, 8)
    ]
    for side, start in ((0, 256), (1, 0), (1, 64), (0, 320), (1, 128)):
        p_copies.append(send_part(side, start, 64))
    for copy in z_copies:
        copy.wait()
    total = zsum[z]
    for k in range(7):
        total += zrecv[k].astype(jnp.float32)
    ysend[...] = total
    y_copy = send(YY, ysend, yrecv, other_y)
    p_copies.append(send_part(1, 192, 64))
    y_copy.wait()
    allg[core, x, z] = (ysend[...] + yrecv[...]).astype(jnp.bfloat16)
    zg = [
        send(ZG + k - 1, allg.at[core, x, z], allg.at[core, x, z], zs[k - 1]) for k in range(1, 8)
    ]
    for start in (256, 320):
        p_copies.append(send_part(1, start, 64))
    for copy in zg:
        copy.wait()
    xg = [send(XG + k - 1, allg.at[core, x], allg.at[core, x], xs[k - 1]) for k in range(1, 4)]
    cg = [send(CG, allg.at[core, x], allg.at[core, x], twin)]
    for k in range(1, 4):
        xg[k - 1].wait()
        there = (x + 4 - k) % 4
        cg.append(send(CG + k, allg.at[core, there], allg.at[core, there], twin))
    for copy in p_copies:
        copy.wait()
    for kind, acc, out, factor in ((0, kacc, dk_out, SCALE), (1, vacc, dv_out, 1.0)):
        grad = acc[pl.ds(ROWS, ROWS), :] + precv[0, kind].astype(jnp.float32)
        grad += precv[1, kind].astype(jnp.float32)
        out[...] = (grad * factor).astype(jnp.bfloat16)
    for copy in cg:
        copy.wait()
    for kind, out, factor in ((0, tk_out, SCALE), (1, tv_out, 1.0)):
        for xi in range(4):
            for n in range(8):
                piece = allg[kind, xi, n].astype(jnp.float32) * factor
                out[pl.ds(xi * 64 + n // 2 * 16, 16), pl.ds(n % 2 * 384, 384)] = piece


def finish(*refs):
    sems = refs[10]
    copies = [pltpu.make_async_copy(refs[n], refs[n + 5], sems.at[n]) for n in range(5)]
    for copy in copies:
        copy.start()
    for copy in copies:
        copy.wait()


def per_device(queries, video_keys, video_values, prompt_keys, prompt_values, out_grad, out_weight, windows, counts):
    f32, bf16 = jnp.float32, jnp.bfloat16
    hbm = pl.BlockSpec(memory_space=pl.ANY)
    smem = pl.BlockSpec(memory_space=pltpu.SMEM)
    vmem = pl.BlockSpec(memory_space=pltpu.VMEM)
    V = pltpu.VMEM
    results = [((ROWS, WIDTH), bf16)] * 3 + [((TEXT, WIDTH), f32)] * 2
    held = pl.pallas_call(
        kernel,
        out_shape=[V(*r) for r in results],
        in_specs=[smem, smem] + [hbm] * 7,
        out_specs=[vmem] * 5,
        scratch_shapes=[
            V((ROWS, WIDTH), bf16),
            V((3 * ROWS + TEXT, WIDTH), bf16),
            V((3 * ROWS + TEXT, WIDTH), bf16),
            V((ROWS, HALF), bf16),
            V((ROWS, HALF), bf16),
            V((WIDTH, HALF), bf16),
            V((WIDTH, HALF), bf16),
            V((ROWS, WIDTH), f32),
            V((ROWS, WIDTH), bf16),
            V((3 * HEADS, KEYS, HD), f32),
            V((3 * HEADS, 8, HD), f32),
            V((KEYS, HD), f32),
            V((HEADS, KEYS, HD), bf16),
            V((HEADS, KEYS, HD), bf16),
            V((3 * ROWS, WIDTH), f32),
            V((3 * ROWS, WIDTH), f32),
            V((2, TEXT, WIDTH), f32),
            V((TEXT, WIDTH), bf16),
            V((TEXT, WIDTH), bf16),
            V((TEXT, WIDTH), f32),
            V((TEXT, WIDTH), bf16),
            V((3, 64, WIDTH), bf16),
            V((8, 16, 384), f32),
            V((8, 16, 384), bf16),
            V((7, 16, 384), bf16),
            V((16, 384), f32),
            V((16, 384), f32),
            V((2, 4, 8, 16, 384), bf16),
            V((2, 2, ROWS, WIDTH), bf16),
            V((2, 2, ROWS, WIDTH), bf16),
            pltpu.SemaphoreType.DMA((8,)),
            pltpu.SemaphoreType.DMA((SLOTS,)),
            pltpu.SemaphoreType.DMA((SLOTS,)),
        ],
        compiler_params=pltpu.CompilerParams(
            collective_id=0, has_side_effects=True, vmem_limit_bytes=54 << 20
        ),
        name="step",
    )(windows.T, counts, queries, video_keys, video_values, prompt_keys, prompt_values, out_grad, out_weight)
    return pl.pallas_call(
        finish,
        out_shape=[jax.ShapeDtypeStruct(*r) for r in results],
        in_specs=[vmem] * 5,
        out_specs=[hbm] * 5,
        scratch_shapes=[pltpu.SemaphoreType.DMA((5,))],
        name="finish",
    )(*[pltpu.with_memory_space_constraint(h, pltpu.VMEM) for h in held])


def solution(mesh):
    both = P("tm", "head")
    text = P(None, "head")
    return jax.shard_map(
        per_device,
        mesh=mesh,
        in_specs=(both, both, both, text, text, both, P("head", None), P(None, None), P(None)),
        out_specs=(both, both, both, text, text),
        check_vma=False,
    )
```

```python
import jax
import jax.numpy as jnp
from jax import lax
from jax.experimental import pallas as pl
from jax.experimental.pallas import tpu as pltpu
from jax.sharding import PartitionSpec as P

HD = 128
PAIR = 2 * HD
TILE = 128
HEADS = 6
ROWS = 384
WIDTH = HEADS * HD
TEXT = 256
HALF = 1536
SEEN = 7 * TILE
KEYS = 9 * TILE
NEG = -1e30
SCALE = HD**-0.5
MESH = pl.DeviceIdType.MESH

OG, KV, PP, TT = 0, 3, 7, 17
CC, XX, ZZ, YY, ZG, XG, CG, STEPS = 0, 1, 4, 11, 12, 19, 22, 26
GROUPS = 3
SLOTS = TT + GROUPS * STEPS


def nt(a, b):
    return lax.dot_general(a, b, (((1,), (1,)), ((), ())), preferred_element_type=jnp.float32)


def tn(a, b):
    return lax.dot_general(a, b, (((0,), (0,)), ((), ())), preferred_element_type=jnp.float32)


def nn(a, b):
    return jnp.dot(a, b, preferred_element_type=jnp.float32)


def folded(x, op):
    return op(x.reshape(TILE // 8, 8, HD), axis=0)


def kernel(
    windows, counts, q_in, k_in, v_in, pk_in, pv_in, og_in, w_in,
    dq_out, dk_out, dv_out, tk_out, tv_out,
    qbuf, kbuf, vbuf, ogown, ogoth, wown, woth, gpart, gbuf, prob, inv, dp, half, dsc, kacc, vacc, tacc,
    csend, crecv, tsum, xsend, xrecv, zsum, zsend, zrecv, ysend, yrecv, allg, psend, precv,
    loc, ssem, rsem,
):
    tm, head = lax.axis_index("tm"), lax.axis_index("head")
    core, x, z, y = tm % 2, (tm // 2) % 4, (tm // 8) % 8, tm // 64

    def at(y_, z_, x_):
        return (((y_ * 8 + z_) * 4 + x_) * 2 + core, head)

    partner = (tm, 1 - head)
    before, after = ((tm + 127) % 128, head), ((tm + 1) % 128, head)
    twin = (tm + 1 - 2 * core, head)
    xs = [at(y, z, (x + k) % 4) for k in range(1, 4)]
    zs = [at(y, (z + k) % 8, x) for k in range(1, 8)]
    other_y = at(1 - y, z, x)

    def local(n, src, dst):
        copy = pltpu.make_async_copy(src, dst, loc.at[n])
        copy.start()
        return copy

    def send(n, src, dst, device):
        copy = pltpu.make_async_remote_copy(
            src_ref=src, dst_ref=dst, send_sem=ssem.at[n], recv_sem=rsem.at[n],
            device_id=device, device_id_type=MESH,
        )
        copy.start()
        return copy

    mine = pl.ds(pl.multiple_of(head * HALF, HALF), HALF)
    theirs = pl.ds(pl.multiple_of((1 - head) * HALF, HALF), HALF)
    l_og = local(0, og_in, ogown)
    l_w = local(1, w_in.at[:, mine], wown)
    l_q = local(2, q_in, qbuf)
    l_k = local(3, k_in, kbuf.at[pl.ds(ROWS, ROWS)])
    l_pk = local(4, pk_in, kbuf.at[pl.ds(3 * ROWS, TEXT)])
    l_v = local(5, v_in, vbuf.at[pl.ds(ROWS, ROWS)])
    l_pv = local(6, pv_in, vbuf.at[pl.ds(3 * ROWS, TEXT)])
    l_w2 = local(7, w_in.at[:, theirs], woth)

    barrier = pltpu.get_barrier_semaphore()
    peers = [partner, before, after, *xs, *zs, other_y]
    for peer in peers:
        pl.semaphore_signal(barrier, inc=1, device_id=peer, device_id_type=MESH)
    pl.semaphore_wait(barrier, len(peers))

    ogs = [
        send(OG + i, og_in.at[pl.ds(i * TILE, TILE)], ogoth.at[pl.ds(i * TILE, TILE)], partner)
        for i in range(3)
    ]
    kvs = [
        send(KV + 0, k_in, kbuf.at[pl.ds(0, ROWS)], after),
        send(KV + 1, k_in, kbuf.at[pl.ds(2 * ROWS, ROWS)], before),
        send(KV + 2, v_in, vbuf.at[pl.ds(0, ROWS)], after),
        send(KV + 3, v_in, vbuf.at[pl.ds(2 * ROWS, ROWS)], before),
    ]

    kacc[...] = jnp.zeros_like(kacc)
    vacc[...] = jnp.zeros_like(vacc)
    tacc[...] = jnp.zeros_like(tacc)

    l_og.wait()
    l_w.wait()

    def project_own(h, carry):
        cols = pl.ds(pl.multiple_of(h * PAIR, PAIR), PAIR)
        gpart[:, cols] = nt(ogown[...], wown[cols, :])
        return carry

    lax.fori_loop(0, HEADS // 2, project_own, 0)

    for copy in (l_q, l_k, l_pk):
        copy.wait()
    kvs[0].wait()
    kvs[1].wait()

    def weights(n, carry):
        i, h = n // HEADS, n % HEADS
        cols = pl.ds(pl.multiple_of(h * HD, HD), HD)
        q = qbuf[pl.ds(pl.multiple_of(i * TILE, TILE), TILE), cols]
        back, ahead, count = windows[0, tm * 3 + i], windows[1, tm * 3 + i], counts[tm * 3 + i]
        prob[n, pl.ds(0, SEEN), :] = nt(kbuf[pl.ds(pl.multiple_of(i * TILE, TILE), SEEN), cols], q)
        prob[n, pl.ds(SEEN, TEXT), :] = nt(kbuf[pl.ds(3 * ROWS, TEXT), cols], q)
        row = lax.broadcasted_iota(jnp.int32, (TILE, HD), 0)
        biases = []
        top = jnp.full((8, HD), NEG, jnp.float32)
        for j in range(9):
            block = prob[n, pl.ds(j * TILE, TILE), :]
            if j < 7:
                bias = jnp.where((j - 3 >= -back) & (j - 3 <= ahead), 0.0, NEG).astype(jnp.float32)
                biases.append(bias)
                top = jnp.maximum(top, folded(block, jnp.max) + bias)
            else:
                block = jnp.where(row + (j - 7) * TILE < count, block, NEG)
                prob[n, pl.ds(j * TILE, TILE), :] = block
                top = jnp.maximum(top, folded(block, jnp.max))
        top = jnp.max(top, axis=0, keepdims=True)
        total = jnp.zeros((8, HD), jnp.float32)
        for j in range(9):
            shift = top - biases[j] if j < 7 else top
            weight = jnp.exp((prob[n, pl.ds(j * TILE, TILE), :] - shift) * SCALE)
            prob[n, pl.ds(j * TILE, TILE), :] = weight
            total += folded(weight, jnp.sum)
        inv[n] = jnp.broadcast_to(1.0 / jnp.sum(total, axis=0, keepdims=True), (8, HD))
        return carry

    lax.fori_loop(0, 3 * HEADS, weights, 0)

    for copy in (l_v, l_pv, l_w2):
        copy.wait()
    kvs[2].wait()
    kvs[3].wait()

    def project_rest(i, h):
        rows = pl.ds(i * TILE, TILE)
        cols = pl.ds(pl.multiple_of(h * PAIR, PAIR), PAIR)
        g = gpart[rows, cols] + nt(ogoth[rows, :], woth[cols, :])
        gbuf[rows, cols] = g.astype(jnp.bfloat16)

    def scores_back(i, h):
        n = i * HEADS + h
        rows = pl.ds(i * TILE, TILE)
        cols = pl.ds(pl.multiple_of(h * HD, HD), HD)
        g = gbuf[rows, cols]
        dp[pl.ds(0, SEEN), :] = nt(vbuf[pl.ds(i * TILE, SEEN), cols], g)
        dp[pl.ds(SEEN, TEXT), :] = nt(vbuf[pl.ds(3 * ROWS, TEXT), cols], g)
        scale = inv[n][0:1]
        delta = jnp.zeros((8, HD), jnp.float32)
        for j in range(9):
            part = pl.ds(j * TILE, TILE)
            p = prob[n, part, :] * scale
            prob[n, part, :] = p
            p16 = p.astype(jnp.bfloat16)
            half[h, part, :] = p16
            delta += folded(p16.astype(jnp.float32) * dp[part, :], jnp.sum)
        delta = jnp.sum(delta, axis=0, keepdims=True)
        for j in range(9):
            part = pl.ds(j * TILE, TILE)
            dsc[h, part, :] = (prob[n, part, :] * (dp[part, :] - delta)).astype(jnp.bfloat16)
        tacc[0, :, cols] += nn(dsc[h, pl.ds(SEEN, TEXT), :], qbuf[rows, cols])
        tacc[1, :, cols] += nn(half[h, pl.ds(SEEN, TEXT), :], g)

    def grads_back(i, h):
        rows = pl.ds(i * TILE, TILE)
        cols = pl.ds(pl.multiple_of(h * HD, HD), HD)
        seen = pl.ds(i * TILE, SEEN)
        vacc[seen, cols] += nn(half[h, pl.ds(0, SEEN), :], gbuf[rows, cols])
        kacc[seen, cols] += nn(dsc[h, pl.ds(0, SEEN), :], qbuf[rows, cols])
        grad = tn(dsc[h, pl.ds(0, SEEN), :], kbuf[seen, cols])
        grad += tn(dsc[h, pl.ds(SEEN, TEXT), :], kbuf[pl.ds(3 * ROWS, TEXT), cols])
        dq_out[rows, cols] = (grad * SCALE).astype(jnp.bfloat16)

    def each_head(step, i, first=0, last=HEADS):
        def body(h, carry):
            step(i, h)
            return carry

        lax.fori_loop(first, last, body, 0)

    p_copies = []

    def pack(side, source, start, count):
        for kind, acc in ((0, kacc), (1, vacc)):
            psend[side, kind, pl.ds(start, count), :] = acc[pl.ds(source, count), :].astype(jnp.bfloat16)

    def send_part(side, start, count):
        part = pl.ds(start, count)
        return send(
            PP + len(p_copies), psend.at[side, :, part], precv.at[side, :, part], after if side else before
        )

    for i in range(2):
        ogs[i].wait()
        each_head(project_rest, i, 0, HEADS // 2)
        each_head(scores_back, i)
        each_head(grads_back, i)
        pack(0, i * TILE, i * TILE, TILE)
        p_copies.append(send_part(0, i * TILE, TILE))

    def text_send(g, step, src, dst, device):
        return send(TT + g * STEPS + step, src, dst, device)

    groups = range(GROUPS)
    ogs[2].wait()
    each_head(project_rest, 2, 0, HEADS // 2)
    c_copies = []
    for g in groups:
        each_head(scores_back, 2, 2 * g, 2 * g + 2)
        csend[g] = tacc[1 - core, :, pl.ds(g * PAIR, PAIR)].astype(jnp.bfloat16)
        c_copies.append(text_send(g, CC, csend.at[g], crecv.at[g], twin))
    x_copies = []
    for g in groups:
        if g == 2:
            each_head(grads_back, 2, 0, 2)
        c_copies[g].wait()
        total = tacc[core, :, pl.ds(g * PAIR, PAIR)] + crecv[g].astype(jnp.float32)
        tsum[g] = total
        xsend[g] = total.astype(jnp.bfloat16)
        x_copies.append([
            text_send(
                g,
                XX + k - 1,
                xsend.at[g, pl.ds(pl.multiple_of((x + k) % 4 * 64, 64), 64)],
                xrecv.at[g, k - 1],
                xs[k - 1],
            )
            for k in range(1, 4)
        ])
    each_head(grads_back, 2, 2, HEADS)
    pack(1, 2 * ROWS, 0, ROWS)
    pack(0, 2 * TILE, 2 * TILE, TILE)
    for side, start in ((1, 0), (0, 256), (1, 64), (0, 320)):
        p_copies.append(send_part(side, start, 64))
    z_copies = []
    for g in groups:
        for copy in x_copies[g]:
            copy.wait()
        total = tsum[g, pl.ds(pl.multiple_of(x * 64, 64), 64), :]
        for k in range(3):
            total += xrecv[g, k].astype(jnp.float32)
        for n in range(8):
            piece = total[n // 2 * 16 : n // 2 * 16 + 16, n % 2 * HD : n % 2 * HD + HD]
            zsum[g, n] = piece
            zsend[g, n] = piece.astype(jnp.bfloat16)
        z_copies.append([
            text_send(g, ZZ + k - 1, zsend.at[g, (z + k) % 8], zrecv.at[g, k - 1], zs[k - 1])
            for k in range(1, 8)
        ])
    p_copies.append(send_part(1, 128, 64))
    y_copies = []
    for g in groups:
        for copy in z_copies[g]:
            copy.wait()
        total = zsum[g, z]
        for k in range(7):
            total += zrecv[g, k].astype(jnp.float32)
        ysend[g] = total
        y_copies.append(text_send(g, YY, ysend.at[g], yrecv.at[g], other_y))
    p_copies.append(send_part(1, 192, 64))
    zg = []
    for g in groups:
        y_copies[g].wait()
        own = allg.at[g, core, x, z]
        own[...] = (ysend[g] + yrecv[g]).astype(jnp.bfloat16)
        zg.append([text_send(g, ZG + k - 1, own, own, zs[k - 1]) for k in range(1, 8)])
    for start in (256, 320):
        p_copies.append(send_part(1, start, 64))
    xg, cg = [], []
    for g in groups:
        for copy in zg[g]:
            copy.wait()
        own = allg.at[g, core, x]
        xg.append([text_send(g, XG + k - 1, own, own, xs[k - 1]) for k in range(1, 4)])
        cg.append([text_send(g, CG, own, own, twin)])
    for g in groups:
        for k in range(1, 4):
            xg[g][k - 1].wait()
            there = allg.at[g, core, (x + 4 - k) % 4]
            cg[g].append(text_send(g, CG + k, there, there, twin))
    for copy in p_copies:
        copy.wait()
    for kind, acc, out, factor in ((0, kacc, dk_out, SCALE), (1, vacc, dv_out, 1.0)):
        grad = acc[pl.ds(ROWS, ROWS), :] + precv[0, kind].astype(jnp.float32)
        grad += precv[1, kind].astype(jnp.float32)
        out[...] = (grad * factor).astype(jnp.bfloat16)
    for g in groups:
        for copy in cg[g]:
            copy.wait()
        for kind, out, factor in ((0, tk_out, SCALE), (1, tv_out, 1.0)):
            for xi in range(4):
                for n in range(8):
                    piece = allg[g, kind, xi, n].astype(jnp.float32) * factor
                    out[pl.ds(xi * 64 + n // 2 * 16, 16), pl.ds(g * PAIR + n % 2 * HD, HD)] = piece


def finish(*refs):
    sems = refs[10]
    copies = [pltpu.make_async_copy(refs[n], refs[n + 5], sems.at[n]) for n in range(5)]
    for copy in copies:
        copy.start()
    for copy in copies:
        copy.wait()


def per_device(queries, video_keys, video_values, prompt_keys, prompt_values, out_grad, out_weight, windows, counts):
    f32, bf16 = jnp.float32, jnp.bfloat16
    hbm = pl.BlockSpec(memory_space=pl.ANY)
    smem = pl.BlockSpec(memory_space=pltpu.SMEM)
    vmem = pl.BlockSpec(memory_space=pltpu.VMEM)
    V = pltpu.VMEM
    results = [((ROWS, WIDTH), bf16)] * 3 + [((TEXT, WIDTH), f32)] * 2
    held = pl.pallas_call(
        kernel,
        out_shape=[V(*r) for r in results],
        in_specs=[smem, smem] + [hbm] * 7,
        out_specs=[vmem] * 5,
        scratch_shapes=[
            V((ROWS, WIDTH), bf16),
            V((3 * ROWS + TEXT, WIDTH), bf16),
            V((3 * ROWS + TEXT, WIDTH), bf16),
            V((ROWS, HALF), bf16),
            V((ROWS, HALF), bf16),
            V((WIDTH, HALF), bf16),
            V((WIDTH, HALF), bf16),
            V((ROWS, WIDTH), f32),
            V((ROWS, WIDTH), bf16),
            V((3 * HEADS, KEYS, HD), f32),
            V((3 * HEADS, 8, HD), f32),
            V((KEYS, HD), f32),
            V((HEADS, KEYS, HD), bf16),
            V((HEADS, KEYS, HD), bf16),
            V((3 * ROWS, WIDTH), f32),
            V((3 * ROWS, WIDTH), f32),
            V((2, TEXT, WIDTH), f32),
            V((GROUPS, TEXT, PAIR), bf16),
            V((GROUPS, TEXT, PAIR), bf16),
            V((GROUPS, TEXT, PAIR), f32),
            V((GROUPS, TEXT, PAIR), bf16),
            V((GROUPS, 3, 64, PAIR), bf16),
            V((GROUPS, 8, 16, HD), f32),
            V((GROUPS, 8, 16, HD), bf16),
            V((GROUPS, 7, 16, HD), bf16),
            V((GROUPS, 16, HD), f32),
            V((GROUPS, 16, HD), f32),
            V((GROUPS, 2, 4, 8, 16, HD), bf16),
            V((2, 2, ROWS, WIDTH), bf16),
            V((2, 2, ROWS, WIDTH), bf16),
            pltpu.SemaphoreType.DMA((8,)),
            pltpu.SemaphoreType.DMA((SLOTS,)),
            pltpu.SemaphoreType.DMA((SLOTS,)),
        ],
        compiler_params=pltpu.CompilerParams(
            collective_id=0, has_side_effects=True, vmem_limit_bytes=54 << 20
        ),
        name="step",
    )(windows.T, counts, queries, video_keys, video_values, prompt_keys, prompt_values, out_grad, out_weight)
    return pl.pallas_call(
        finish,
        out_shape=[jax.ShapeDtypeStruct(*r) for r in results],
        in_specs=[vmem] * 5,
        out_specs=[hbm] * 5,
        scratch_shapes=[pltpu.SemaphoreType.DMA((5,))],
        name="finish",
    )(*[pltpu.with_memory_space_constraint(h, pltpu.VMEM) for h in held])


def solution(mesh):
    both = P("tm", "head")
    text = P(None, "head")
    return jax.shard_map(
        per_device,
        mesh=mesh,
        in_specs=(both, both, both, text, text, both, P("head", None), P(None, None), P(None)),
        out_specs=(both, both, both, text, text),
        check_vma=False,
    )
```

```python
import jax
import jax.numpy as jnp
from jax import lax
from jax.experimental import pallas as pl
from jax.experimental.pallas import tpu as pltpu
from jax.sharding import PartitionSpec as P

HD = 128
PAIR = 2 * HD
TILE = 128
HEADS = 6
ROWS = 384
WIDTH = HEADS * HD
TEXT = 256
HALF = 1536
SEEN = 7 * TILE
KEYS = 9 * TILE
NEG = -1e30
SCALE = HD**-0.5
MESH = pl.DeviceIdType.MESH

OG, KV, PP, TT = 0, 3, 7, 17
CC, XX, ZZ, YY, ZG, XG, CG, STEPS = 0, 1, 4, 11, 12, 19, 22, 26
GROUPS = 3
SLOTS = TT + GROUPS * STEPS


def nt(a, b):
    return lax.dot_general(a, b, (((1,), (1,)), ((), ())), preferred_element_type=jnp.float32)


def tn(a, b):
    return lax.dot_general(a, b, (((0,), (0,)), ((), ())), preferred_element_type=jnp.float32)


def nn(a, b):
    return jnp.dot(a, b, preferred_element_type=jnp.float32)


def folded(x, op):
    return op(x.reshape(TILE // 8, 8, HD), axis=0)


def kernel(
    windows, counts, q_in, k_in, v_in, pk_in, pv_in, og_in, w_in,
    dq_out, dk_out, dv_out, tk_out, tv_out,
    qbuf, kbuf, vbuf, ogown, ogoth, wown, woth, gpart, gbuf, prob, inv, dp, half, dsc, kacc, vacc, tacc,
    csend, crecv, tsum, xsend, xrecv, zsum, zsend, zrecv, ysend, yrecv, allg, psend, precv,
    loc, ssem, rsem,
):
    tm, head = lax.axis_index("tm"), lax.axis_index("head")
    core, x, z, y = tm % 2, (tm // 2) % 4, (tm // 8) % 8, tm // 64

    def at(y_, z_, x_):
        return (((y_ * 8 + z_) * 4 + x_) * 2 + core, head)

    partner = (tm, 1 - head)
    before, after = ((tm + 127) % 128, head), ((tm + 1) % 128, head)
    twin = (tm + 1 - 2 * core, head)
    xs = [at(y, z, (x + k) % 4) for k in range(1, 4)]
    zs = [at(y, (z + k) % 8, x) for k in range(1, 8)]
    other_y = at(1 - y, z, x)

    def local(n, src, dst):
        copy = pltpu.make_async_copy(src, dst, loc.at[n])
        copy.start()
        return copy

    def send(n, src, dst, device):
        copy = pltpu.make_async_remote_copy(
            src_ref=src, dst_ref=dst, send_sem=ssem.at[n], recv_sem=rsem.at[n],
            device_id=device, device_id_type=MESH,
        )
        copy.start()
        return copy

    mine = pl.ds(pl.multiple_of(head * HALF, HALF), HALF)
    theirs = pl.ds(pl.multiple_of((1 - head) * HALF, HALF), HALF)
    l_og = local(0, og_in, ogown)
    l_w = local(1, w_in.at[:, mine], wown)
    l_q = local(2, q_in, qbuf)
    l_k = local(3, k_in, kbuf.at[pl.ds(ROWS, ROWS)])
    l_pk = local(4, pk_in, kbuf.at[pl.ds(3 * ROWS, TEXT)])
    l_v = local(5, v_in, vbuf.at[pl.ds(ROWS, ROWS)])
    l_pv = local(6, pv_in, vbuf.at[pl.ds(3 * ROWS, TEXT)])
    l_w2 = local(7, w_in.at[:, theirs], woth)

    barrier = pltpu.get_barrier_semaphore()
    peers = [partner, before, after, *xs, *zs, other_y]
    for peer in peers:
        pl.semaphore_signal(barrier, inc=1, device_id=peer, device_id_type=MESH)
    pl.semaphore_wait(barrier, len(peers))

    ogs = [
        send(OG + i, og_in.at[pl.ds(i * TILE, TILE)], ogoth.at[pl.ds(i * TILE, TILE)], partner)
        for i in (0, 2, 1)
    ]
    kvs = [
        send(KV + 0, k_in, kbuf.at[pl.ds(0, ROWS)], after),
        send(KV + 1, k_in, kbuf.at[pl.ds(2 * ROWS, ROWS)], before),
        send(KV + 2, v_in, vbuf.at[pl.ds(0, ROWS)], after),
        send(KV + 3, v_in, vbuf.at[pl.ds(2 * ROWS, ROWS)], before),
    ]

    kacc[...] = jnp.zeros_like(kacc)
    vacc[...] = jnp.zeros_like(vacc)
    tacc[...] = jnp.zeros_like(tacc)

    l_og.wait()
    l_w.wait()

    def project_own(h, carry):
        cols = pl.ds(pl.multiple_of(h * PAIR, PAIR), PAIR)
        gpart[:, cols] = nt(ogown[...], wown[cols, :])
        return carry

    lax.fori_loop(0, HEADS // 2, project_own, 0)

    for copy in (l_q, l_k, l_pk):
        copy.wait()
    kvs[0].wait()
    kvs[1].wait()

    def weights(n, carry):
        i, h = n // HEADS, n % HEADS
        cols = pl.ds(pl.multiple_of(h * HD, HD), HD)
        q = qbuf[pl.ds(pl.multiple_of(i * TILE, TILE), TILE), cols]
        back, ahead, count = windows[0, tm * 3 + i], windows[1, tm * 3 + i], counts[tm * 3 + i]
        prob[n, pl.ds(0, SEEN), :] = nt(kbuf[pl.ds(pl.multiple_of(i * TILE, TILE), SEEN), cols], q)
        prob[n, pl.ds(SEEN, TEXT), :] = nt(kbuf[pl.ds(3 * ROWS, TEXT), cols], q)
        row = lax.broadcasted_iota(jnp.int32, (TILE, HD), 0)
        biases = []
        top = jnp.full((8, HD), NEG, jnp.float32)
        for j in range(9):
            block = prob[n, pl.ds(j * TILE, TILE), :]
            if j < 7:
                bias = jnp.where((j - 3 >= -back) & (j - 3 <= ahead), 0.0, NEG).astype(jnp.float32)
                biases.append(bias)
                top = jnp.maximum(top, folded(block, jnp.max) + bias)
            else:
                block = jnp.where(row + (j - 7) * TILE < count, block, NEG)
                prob[n, pl.ds(j * TILE, TILE), :] = block
                top = jnp.maximum(top, folded(block, jnp.max))
        top = jnp.max(top, axis=0, keepdims=True)
        total = jnp.zeros((8, HD), jnp.float32)
        for j in range(9):
            shift = top - biases[j] if j < 7 else top
            weight = jnp.exp((prob[n, pl.ds(j * TILE, TILE), :] - shift) * SCALE)
            prob[n, pl.ds(j * TILE, TILE), :] = weight
            total += folded(weight, jnp.sum)
        inv[n] = jnp.broadcast_to(1.0 / jnp.sum(total, axis=0, keepdims=True), (8, HD))
        return carry

    lax.fori_loop(0, 3 * HEADS, weights, 0)

    for copy in (l_v, l_pv, l_w2):
        copy.wait()
    kvs[2].wait()
    kvs[3].wait()

    def project_rest(i, h):
        rows = pl.ds(i * TILE, TILE)
        cols = pl.ds(pl.multiple_of(h * PAIR, PAIR), PAIR)
        g = gpart[rows, cols] + nt(ogoth[rows, :], woth[cols, :])
        gbuf[rows, cols] = g.astype(jnp.bfloat16)

    def scores_back(i, h):
        n = i * HEADS + h
        rows = pl.ds(i * TILE, TILE)
        cols = pl.ds(pl.multiple_of(h * HD, HD), HD)
        g = gbuf[rows, cols]
        dp[pl.ds(0, SEEN), :] = nt(vbuf[pl.ds(i * TILE, SEEN), cols], g)
        dp[pl.ds(SEEN, TEXT), :] = nt(vbuf[pl.ds(3 * ROWS, TEXT), cols], g)
        scale = inv[n][0:1]
        delta = jnp.zeros((8, HD), jnp.float32)
        for j in range(9):
            part = pl.ds(j * TILE, TILE)
            p = prob[n, part, :] * scale
            prob[n, part, :] = p
            p16 = p.astype(jnp.bfloat16)
            half[h, part, :] = p16
            delta += folded(p16.astype(jnp.float32) * dp[part, :], jnp.sum)
        delta = jnp.sum(delta, axis=0, keepdims=True)
        for j in range(9):
            part = pl.ds(j * TILE, TILE)
            dsc[h, part, :] = (prob[n, part, :] * (dp[part, :] - delta)).astype(jnp.bfloat16)
        tacc[0, :, cols] += nn(dsc[h, pl.ds(SEEN, TEXT), :], qbuf[rows, cols])
        tacc[1, :, cols] += nn(half[h, pl.ds(SEEN, TEXT), :], g)

    def grads_back(i, h):
        rows = pl.ds(i * TILE, TILE)
        cols = pl.ds(pl.multiple_of(h * HD, HD), HD)
        seen = pl.ds(i * TILE, SEEN)
        vacc[seen, cols] += nn(half[h, pl.ds(0, SEEN), :], gbuf[rows, cols])
        kacc[seen, cols] += nn(dsc[h, pl.ds(0, SEEN), :], qbuf[rows, cols])
        grad = tn(dsc[h, pl.ds(0, SEEN), :], kbuf[seen, cols])
        grad += tn(dsc[h, pl.ds(SEEN, TEXT), :], kbuf[pl.ds(3 * ROWS, TEXT), cols])
        dq_out[rows, cols] = (grad * SCALE).astype(jnp.bfloat16)

    def each_head(step, i, first=0, last=HEADS):
        def body(h, carry):
            step(i, h)
            return carry

        lax.fori_loop(first, last, body, 0)

    p_copies = []

    def pack(side, source, start, count):
        for kind, acc in ((0, kacc), (1, vacc)):
            psend[side, kind, pl.ds(start, count), :] = acc[pl.ds(source, count), :].astype(jnp.bfloat16)

    def send_part(side, start, count):
        part = pl.ds(start, count)
        return send(
            PP + len(p_copies), psend.at[side, :, part], precv.at[side, :, part], after if side else before
        )

    for turn, i in enumerate((0, 2)):
        ogs[turn].wait()
        each_head(project_rest, i, 0, HEADS // 2)
        each_head(scores_back, i)
        each_head(grads_back, i)
        pack(turn, turn * 2 * ROWS + i * TILE, i * TILE, TILE)
        p_copies.append(send_part(turn, i * TILE, TILE))

    def text_send(g, step, src, dst, device):
        return send(TT + g * STEPS + step, src, dst, device)

    groups = range(GROUPS)
    ogs[2].wait()
    each_head(project_rest, 1, 0, HEADS // 2)
    c_copies = []
    for g in groups:
        each_head(scores_back, 1, 2 * g, 2 * g + 2)
        csend[g] = tacc[1 - core, :, pl.ds(g * PAIR, PAIR)].astype(jnp.bfloat16)
        c_copies.append(text_send(g, CC, csend.at[g], crecv.at[g], twin))
    x_copies = []
    for g in groups:
        if g == 2:
            each_head(grads_back, 1, 0, 2)
        c_copies[g].wait()
        total = tacc[core, :, pl.ds(g * PAIR, PAIR)] + crecv[g].astype(jnp.float32)
        tsum[g] = total
        xsend[g] = total.astype(jnp.bfloat16)
        x_copies.append([
            text_send(
                g,
                XX + k - 1,
                xsend.at[g, pl.ds(pl.multiple_of((x + k) % 4 * 64, 64), 64)],
                xrecv.at[g, k - 1],
                xs[k - 1],
            )
            for k in range(1, 4)
        ])
    each_head(grads_back, 1, 2, HEADS)
    pack(0, TILE, TILE, 2 * TILE)
    pack(1, 2 * ROWS, 0, 2 * TILE)
    for side, start in ((0, 128), (1, 0), (0, 192), (1, 64)):
        p_copies.append(send_part(side, start, 64))
    z_copies = []
    for g in groups:
        for copy in x_copies[g]:
            copy.wait()
        total = tsum[g, pl.ds(pl.multiple_of(x * 64, 64), 64), :]
        for k in range(3):
            total += xrecv[g, k].astype(jnp.float32)
        for n in range(8):
            piece = total[n // 2 * 16 : n // 2 * 16 + 16, n % 2 * HD : n % 2 * HD + HD]
            zsum[g, n] = piece
            zsend[g, n] = piece.astype(jnp.bfloat16)
        z_copies.append([
            text_send(g, ZZ + k - 1, zsend.at[g, (z + k) % 8], zrecv.at[g, k - 1], zs[k - 1])
            for k in (4, 3, 5, 2, 6, 1, 7)
        ])
    for side, start in ((0, 256), (1, 128)):
        p_copies.append(send_part(side, start, 64))
    y_copies = []
    for g in groups:
        for copy in z_copies[g]:
            copy.wait()
        total = zsum[g, z]
        for k in range(7):
            total += zrecv[g, k].astype(jnp.float32)
        ysend[g] = total
        y_copies.append(text_send(g, YY, ysend.at[g], yrecv.at[g], other_y))
    for side, start in ((0, 320), (1, 192)):
        p_copies.append(send_part(side, start, 64))
    zg = []
    for g in groups:
        y_copies[g].wait()
        own = allg.at[g, core, x, z]
        own[...] = (ysend[g] + yrecv[g]).astype(jnp.bfloat16)
        zg.append([text_send(g, ZG + k - 1, own, own, zs[k - 1]) for k in (4, 3, 5, 2, 6, 1, 7)])
    xg, cg = [], []
    for g in groups:
        for copy in zg[g]:
            copy.wait()
        own = allg.at[g, core, x]
        xg.append([text_send(g, XG + k - 1, own, own, xs[k - 1]) for k in range(1, 4)])
        cg.append([text_send(g, CG, own, own, twin)])
    for g in groups:
        for k in range(1, 4):
            xg[g][k - 1].wait()
            there = allg.at[g, core, (x + 4 - k) % 4]
            cg[g].append(text_send(g, CG + k, there, there, twin))
    for copy in p_copies:
        copy.wait()
    for kind, acc, out, factor in ((0, kacc, dk_out, SCALE), (1, vacc, dv_out, 1.0)):
        grad = acc[pl.ds(ROWS, ROWS), :] + precv[0, kind].astype(jnp.float32)
        grad += precv[1, kind].astype(jnp.float32)
        out[...] = (grad * factor).astype(jnp.bfloat16)
    for g in groups:
        for copy in cg[g]:
            copy.wait()
        for kind, out, factor in ((0, tk_out, SCALE), (1, tv_out, 1.0)):
            for xi in range(4):
                for n in range(8):
                    piece = allg[g, kind, xi, n].astype(jnp.float32) * factor
                    out[pl.ds(xi * 64 + n // 2 * 16, 16), pl.ds(g * PAIR + n % 2 * HD, HD)] = piece


def finish(*refs):
    sems = refs[10]
    copies = [pltpu.make_async_copy(refs[n], refs[n + 5], sems.at[n]) for n in range(5)]
    for copy in copies:
        copy.start()
    for copy in copies:
        copy.wait()


def per_device(queries, video_keys, video_values, prompt_keys, prompt_values, out_grad, out_weight, windows, counts):
    f32, bf16 = jnp.float32, jnp.bfloat16
    hbm = pl.BlockSpec(memory_space=pl.ANY)
    smem = pl.BlockSpec(memory_space=pltpu.SMEM)
    vmem = pl.BlockSpec(memory_space=pltpu.VMEM)
    V = pltpu.VMEM
    results = [((ROWS, WIDTH), bf16)] * 3 + [((TEXT, WIDTH), f32)] * 2
    held = pl.pallas_call(
        kernel,
        out_shape=[V(*r) for r in results],
        in_specs=[smem, smem] + [hbm] * 7,
        out_specs=[vmem] * 5,
        scratch_shapes=[
            V((ROWS, WIDTH), bf16),
            V((3 * ROWS + TEXT, WIDTH), bf16),
            V((3 * ROWS + TEXT, WIDTH), bf16),
            V((ROWS, HALF), bf16),
            V((ROWS, HALF), bf16),
            V((WIDTH, HALF), bf16),
            V((WIDTH, HALF), bf16),
            V((ROWS, WIDTH), f32),
            V((ROWS, WIDTH), bf16),
            V((3 * HEADS, KEYS, HD), f32),
            V((3 * HEADS, 8, HD), f32),
            V((KEYS, HD), f32),
            V((HEADS, KEYS, HD), bf16),
            V((HEADS, KEYS, HD), bf16),
            V((3 * ROWS, WIDTH), f32),
            V((3 * ROWS, WIDTH), f32),
            V((2, TEXT, WIDTH), f32),
            V((GROUPS, TEXT, PAIR), bf16),
            V((GROUPS, TEXT, PAIR), bf16),
            V((GROUPS, TEXT, PAIR), f32),
            V((GROUPS, TEXT, PAIR), bf16),
            V((GROUPS, 3, 64, PAIR), bf16),
            V((GROUPS, 8, 16, HD), f32),
            V((GROUPS, 8, 16, HD), bf16),
            V((GROUPS, 7, 16, HD), bf16),
            V((GROUPS, 16, HD), f32),
            V((GROUPS, 16, HD), f32),
            V((GROUPS, 2, 4, 8, 16, HD), bf16),
            V((2, 2, ROWS, WIDTH), bf16),
            V((2, 2, ROWS, WIDTH), bf16),
            pltpu.SemaphoreType.DMA((8,)),
            pltpu.SemaphoreType.DMA((SLOTS,)),
            pltpu.SemaphoreType.DMA((SLOTS,)),
        ],
        compiler_params=pltpu.CompilerParams(
            collective_id=0, has_side_effects=True, vmem_limit_bytes=54 << 20
        ),
        name="step",
    )(windows.T, counts, queries, video_keys, video_values, prompt_keys, prompt_values, out_grad, out_weight)
    return pl.pallas_call(
        finish,
        out_shape=[jax.ShapeDtypeStruct(*r) for r in results],
        in_specs=[vmem] * 5,
        out_specs=[hbm] * 5,
        scratch_shapes=[pltpu.SemaphoreType.DMA((5,))],
        name="finish",
    )(*[pltpu.with_memory_space_constraint(h, pltpu.VMEM) for h in held])


def solution(mesh):
    both = P("tm", "head")
    text = P(None, "head")
    return jax.shard_map(
        per_device,
        mesh=mesh,
        in_specs=(both, both, both, text, text, both, P("head", None), P(None, None), P(None)),
        out_specs=(both, both, both, text, text),
        check_vma=False,
    )
```
